32 devices in a mesh: row: 4 (over z), col: 8 (over y, x, core).
Axes of the slice: x: 2, y: 2, z: 4, core: 2. Of those that a mesh axis runs over, the one named last changes fastest.
Arguments:
- spectra: bfloat16 [1024, 32, 128], P(('row', 'col')), may hold values from -6 to 6
- pair_bins: int32 [1024, 1024], P('row', 'col'), may hold values from 0 to 255
- row_subs: int32 [4, 16], P('row'), may hold values from 0 to 31, as said below
- station_subs: int32 [1024, 8], replicated, may hold values from 0 to 31, as said below
- kernel: bfloat16 [32, 256, 256], replicated, may hold values from -0.375 to 0.375
Outputs:
- spectrum: float32 [32, 32, 256], P(('row', 'col'))
The draws below stay inside these ranges and needn't reach their ends.
Inputs may be any that keep to these rules, and one draw needn't show every extreme that they name: `row_subs`: each row lists 16 distinct subarrays; each subarray is listed for exactly two row blocks. `station_subs`: each station names 8 distinct subarrays, all listed in row_subs for the station's row block.
All inputs are finite; a program needn't handle non-finite values.
Results may differ from the reference program's by a relative error of at most 0.0039.
Values may be sent and summed in bfloat16 or wider, within the bound.
A program may use at most 64 MiB of HBM per device.

```python
import jax
import jax.numpy as jnp
from jax import lax

F = 32
WIN2 = 128
NBIN = 256
V = 256
MS = 8
STA = 1024
ROW_STA = 256
NSUB = 32
LS = 16
N_ROW = 4
N_COL = 8


def make_lists(key):
    shuffled = jax.random.permutation(jax.random.fold_in(key, 11), NSUB).astype(jnp.int32)
    half_list = LS // 2
    quarter = half_list // 4
    row_ids = jnp.arange(N_ROW, dtype=jnp.int32)[:, None]
    slot_ids = jnp.arange(LS, dtype=jnp.int32)[None, :]
    inner = slot_ids % half_list
    far_rows = jnp.where(inner < quarter, row_ids + N_ROW - 1, jnp.where(inner < 2 * quarter, row_ids + 1, row_ids + N_ROW // 2)) % N_ROW
    block_ids = jnp.where(slot_ids < half_list, row_ids, far_rows)
    places = block_ids * half_list + inner
    return shuffled[places]


def draw_row_subs(key, part):
    return make_lists(key)


def draw_station_subs(key, part):
    lists = make_lists(key)
    scores = jax.random.randint(jax.random.fold_in(key, 23), (STA, LS), 0, 1 << 20) * LS + jnp.arange(LS, dtype=jnp.int32)[None, :]
    order = jnp.argsort(-scores, axis=1)[:, :MS]
    owners = lists[jnp.arange(STA, dtype=jnp.int32) // ROW_STA]
    return jnp.take_along_axis(owners, order, axis=1).astype(jnp.int32)


def set_ends(drawn, rng, low, high):
    shape = drawn.shape
    index_at = [jax.random.randint(jax.random.fold_in(rng, axis), (), 0, shape[axis]) for axis in range(len(shape))]
    drawn = drawn.at[tuple(index_at)].set(low)
    longest = shape.index(max(shape))
    index_at[longest] = (index_at[longest] + 1) % shape[longest]
    return drawn.at[tuple(index_at)].set(high)


def steps_of(key, dims, cuts, least, largest):
    level, own = 1.0, jax.random.fold_in(key, 6)
    for position, blocks in cuts:
        heights = jnp.exp(jax.random.uniform(jax.random.fold_in(own, position), (blocks,), jnp.float32, least / len(cuts), largest / len(cuts)))
        level = level * jnp.repeat(heights, dims[position] // blocks).reshape([-1 if axis == position else 1 for axis in range(len(dims))])
    return level


def normal_values(rng, extent, spread, most, pieces=(), kind=jnp.bfloat16):
    drawn = jax.random.normal(rng, extent, jnp.float32) * spread
    if len(pieces) > 0:
        drawn = steps_of(rng, extent, pieces, -0.22, 0.18) * drawn
    return jnp.clip(drawn, min=-most, max=most).astype(kind)


def setup_inputs(seed: int = 0) -> dict:
    seeds = jax.random.split(jax.random.key(seed), 6)
    spectra = normal_values(seeds[0], (STA, F, WIN2), 1.0, 6.0, ((0, 32),))
    pair_bins = set_ends(jax.random.randint(seeds[1], (STA, STA), 0, NBIN), jax.random.fold_in(seeds[1], 1), 0, NBIN - 1).astype(jnp.int32)
    row_subs = draw_row_subs(jax.random.fold_in(seeds[5], 71), 0)
    station_subs = draw_station_subs(jax.random.fold_in(seeds[5], 71), 0)
    kernel = normal_values(seeds[4], (F, NBIN, V), NBIN ** -0.5, 0.375)
    return {"spectra": spectra, "pair_bins": pair_bins, "row_subs": row_subs, "station_subs": station_subs, "kernel": kernel}


def reference(spectra, pair_bins, row_subs, station_subs, kernel):
    stations = spectra.shape[0]
    shard_rows = stations // (N_ROW * N_COL)
    row_span = stations // N_ROW
    col_span = stations // N_COL
    slot_count = row_subs.shape[1]
    positions = jnp.arange(col_span, dtype=jnp.int32)
    bin_ids = jnp.arange(NBIN, dtype=jnp.int32)

    def one_block(running, block_index):
        row_block = block_index // N_COL
        col_group = block_index % N_COL
        row_first = (row_block * row_span).astype(jnp.int32)
        row_spectra = lax.dynamic_slice_in_dim(spectra, row_first, row_span, 0).astype(jnp.float32)
        col_ids = ((positions // shard_rows * N_COL + col_group) * shard_rows + positions % shard_rows).astype(jnp.int32)
        col_spectra = jnp.take(spectra, col_ids, axis=0).astype(jnp.float32)
        cross_spec = jnp.einsum('aft,jft->faj', row_spectra, col_spectra, precision=lax.Precision.HIGHEST)
        cross_spec = lax.optimization_barrier(cross_spec.astype(jnp.bfloat16)).astype(jnp.float32)
        bins_block = lax.dynamic_slice(pair_bins, (row_first, (col_group * col_span).astype(jnp.int32)), (row_span, col_span))
        slot_subs = lax.dynamic_index_in_dim(row_subs, row_block.astype(jnp.int32), 0, keepdims=False)
        row_members = lax.dynamic_slice_in_dim(station_subs, row_first, row_span, 0)
        col_members = jnp.take(station_subs, col_ids, axis=0)
        row_mask = jnp.any(row_members[None, :, :] == slot_subs[:, None, None], axis=2).astype(jnp.float32)
        col_mask = jnp.any(col_members[None, :, :] == slot_subs[:, None, None], axis=2).astype(jnp.float32)
        weighted = row_mask[:, None, :, None] * col_mask[:, None, None, :] * cross_spec[None]
        onehot = (bins_block.reshape(-1, 1) == bin_ids[None, :]).astype(jnp.float32)
        partial_value = jnp.dot(weighted.reshape(slot_count * F, row_span * col_span), onehot, precision=lax.Precision.HIGHEST)
        running = running.at[slot_subs].add(partial_value.reshape(slot_count, F, NBIN))
        return (running, None)
    start_sums = jnp.zeros((NSUB, F, NBIN), jnp.float32)
    binned_sum, unused = lax.scan(one_block, start_sums, jnp.arange(N_ROW * N_COL, dtype=jnp.int32))
    binned = lax.optimization_barrier(binned_sum.astype(jnp.bfloat16)).astype(jnp.float32)
    velocity_power = jnp.einsum('sfb,fbv->sfv', binned, kernel.astype(jnp.float32), precision=lax.Precision.HIGHEST)
    scale = lax.rsqrt(lax.optimization_barrier(jnp.mean(velocity_power * velocity_power, axis=2, keepdims=True)) + 1e-06)
    return velocity_power * scale
```

```python
import functools

import jax
import jax.numpy as jnp
from jax import lax
from jax.experimental import pallas as pl
from jax.experimental.pallas import tpu as pltpu
from jax.sharding import PartitionSpec as P

MESH = pl.DeviceIdType.MESH
NT = (((1,), (1,)), ((), ()))
NBIN = 256
PIECES = 4
UNROLL = 8


def gather_kernel(x_ref, row_ref, col_ref, own_sem, row_send, row_recv, sib_send, sib_recv,
                  fwd_send, fwd_recv, col_send, col_recv):
    rows, cols = lax.axis_size("row"), lax.axis_size("col")
    r, c = lax.axis_index("row"), lax.axis_index("col")
    freqs, shard = x_ref.shape[0], x_ref.shape[1]
    pairs = cols // 2
    g, h = c // 2, c % 2
    sib = g * 2 + (1 - h)
    span = freqs // PIECES

    barrier = pltpu.get_barrier_semaphore()
    for d in range(1, pairs):
        pl.semaphore_signal(barrier, inc=1, device_id=(r, lax.rem(g + d, pairs) * 2 + h), device_id_type=MESH)
    pl.semaphore_signal(barrier, inc=1, device_id=(r, sib), device_id_type=MESH)
    for d in range(1, rows):
        pl.semaphore_signal(barrier, inc=1, device_id=(lax.rem(r + d, rows), c), device_id_type=MESH)

    def slot(ref, index, piece):
        return ref.at[pl.ds(piece * span, span), pl.ds(pl.multiple_of(index * shard, shard), shard), :]

    own_row = pltpu.make_async_copy(x_ref, row_ref.at[:, pl.ds(pl.multiple_of(c * shard, shard), shard), :], own_sem.at[0])
    own_col = pltpu.make_async_copy(x_ref, col_ref.at[:, pl.ds(pl.multiple_of(r * shard, shard), shard), :], own_sem.at[1])
    own_row.start()
    own_col.start()
    pl.semaphore_wait(barrier, pairs - 1 + 1 + rows - 1)

    started = []
    row_copies = {}
    for k in range(PIECES):
        piece = x_ref.at[pl.ds(k * span, span)]
        for d in range(1, rows):
            copy = pltpu.make_async_remote_copy(
                piece, slot(col_ref, r, k), col_send.at[d, k], col_recv.at[d, k],
                device_id=(lax.rem(r + d, rows), c), device_id_type=MESH)
            copy.start()
            started.append(copy)
        for d in range(1, pairs):
            copy = pltpu.make_async_remote_copy(
                piece, slot(row_ref, c, k), row_send.at[d, k], row_recv.at[d, k],
                device_id=(r, lax.rem(g + d, pairs) * 2 + h), device_id_type=MESH)
            copy.start()
            row_copies[d, k] = copy
        copy = pltpu.make_async_remote_copy(
            piece, slot(row_ref, c, k), sib_send.at[k], sib_recv.at[k],
            device_id=(r, sib), device_id_type=MESH)
        copy.start()
        started.append(copy)
    for k in range(PIECES):
        for d in range(1, pairs):
            row_copies[d, k].wait_recv()
            source = lax.rem(g - d + pairs, pairs) * 2 + h
            copy = pltpu.make_async_remote_copy(
                slot(row_ref, source, k), slot(row_ref, source, k), fwd_send.at[d, k], fwd_recv.at[d, k],
                device_id=(r, sib), device_id_type=MESH)
            copy.start()
            started.append(copy)
    for copy in row_copies.values():
        copy.wait_send()
    for copy in started:
        copy.wait()
    own_row.wait()
    own_col.wait()


def gather(x):
    rows, cols = lax.axis_size("row"), lax.axis_size("col")
    freqs, shard, width = x.shape
    pairs = cols // 2
    dma = pltpu.SemaphoreType.DMA
    return pl.pallas_call(
        gather_kernel,
        out_shape=(jax.ShapeDtypeStruct((freqs, cols * shard, width), x.dtype),
                   jax.ShapeDtypeStruct((freqs, rows * shard, width), x.dtype)),
        in_specs=[pl.BlockSpec(memory_space=pl.ANY)],
        out_specs=(pl.BlockSpec(memory_space=pl.ANY),) * 2,
        scratch_shapes=[dma((2,)), dma((pairs, PIECES)), dma((pairs, PIECES)), dma((PIECES,)), dma((PIECES,)),
                        dma((pairs, PIECES)), dma((pairs, PIECES)), dma((rows, PIECES)), dma((rows, PIECES))],
        compiler_params=pltpu.CompilerParams(collective_id=0, has_side_effects=True),
        name="gather_spectra",
    )(x)


def bin_kernel(cols, row_ref, col_ref, bins_ref, rmask_ref, cmask_ref, out_ref, cross, w0, o0, w1, o1, acc):
    freqs, span, _ = row_ref.shape
    width = col_ref.shape[1]
    slots = cmask_ref.shape[0]

    def one_freq(f, carry):
        cross[pl.ds(f, span, stride=freqs), :] = lax.dot_general(
            row_ref[f], col_ref[f], NT, preferred_element_type=jnp.float32)
        return carry

    lax.fori_loop(0, freqs, one_freq, 0, unroll=4)
    steps = span // UNROLL

    def build(step, w, o):
        for u in range(UNROLL):
            i = step * UNROLL + u
            block = cross[pl.ds(pl.multiple_of(i * freqs, freqs), freqs), :].astype(jnp.bfloat16)
            mask = rmask_ref[i] * cmask_ref[...]
            weighted = mask[:, None, :] * block[None]
            w[:, u * width:(u + 1) * width] = weighted.reshape(slots * freqs, width)
            ids = lax.broadcasted_iota(jnp.int32, (NBIN, width), 0)
            o[:, u * width:(u + 1) * width] = jnp.where(ids == bins_ref[pl.ds(i, 1), :], 1.0, 0.0).astype(jnp.bfloat16)

    def multiply(w, o):
        acc[...] += lax.dot_general(w[...], o[...], NT, preferred_element_type=jnp.float32)

    acc[...] = jnp.zeros_like(acc)
    build(0, w0, o0)

    def two(pair, carry):
        build(2 * pair + 1, w1, o1)
        multiply(w0, o0)
        build(lax.min(2 * pair + 2, steps - 1), w0, o0)
        multiply(w1, o1)
        return carry

    lax.fori_loop(0, steps // 2, two, 0)
    share = freqs // cols
    for k in range(cols):
        for s in range(slots):
            out_ref[k, s * share:(s + 1) * share, :] = acc[s * freqs + k * share:s * freqs + (k + 1) * share, :]


def bin_pairs(row_spectra, col_spectra, pair_bins, row_mask, col_mask):
    cols = lax.axis_size("col")
    freqs, span, _ = row_spectra.shape
    width = col_spectra.shape[1]
    slots = col_mask.shape[0]
    vmem = pl.BlockSpec(memory_space=pltpu.VMEM)
    return pl.pallas_call(
        functools.partial(bin_kernel, cols),
        out_shape=jax.ShapeDtypeStruct((cols, slots * freqs // cols, NBIN), jnp.float32),
        in_specs=[vmem] * 5,
        out_specs=vmem,
        scratch_shapes=[
            pltpu.VMEM((span * freqs, width), jnp.float32),
            pltpu.VMEM((slots * freqs, UNROLL * width), jnp.bfloat16),
            pltpu.VMEM((NBIN, UNROLL * width), jnp.bfloat16),
            pltpu.VMEM((slots * freqs, UNROLL * width), jnp.bfloat16),
            pltpu.VMEM((NBIN, UNROLL * width), jnp.bfloat16),
            pltpu.VMEM((slots * freqs, NBIN), jnp.float32),
        ],
        name="bin_pairs",
    )(row_spectra, col_spectra, pair_bins, row_mask, col_mask)


def split(x, n):
    if n & (n - 1) == 0:
        return x >> (n.bit_length() - 1), x & (n - 1)
    return lax.div(x, n), lax.rem(x, n)


def finish_kernel(part_ref, subs_ref, kern_ref, out_ref, got1, spread, got2, ready, got3, kern,
                  kern_sem, send1, recv1, send2, recv2, send3, recv3):
    rows, cols = lax.axis_size("row"), lax.axis_size("col")
    r, c = lax.axis_index("row"), lax.axis_index("col")
    share = kern.shape[0]
    freqs = share * cols

    barrier = pltpu.get_barrier_semaphore()
    for d in range(1, cols):
        pl.semaphore_signal(barrier, inc=1, device_id=(r, lax.rem(c + d, cols)), device_id_type=MESH)
    for d in range(1, rows):
        pl.semaphore_signal(barrier, inc=1, device_id=(lax.rem(r + d, rows), c), device_id_type=MESH)
    fetch = pltpu.make_async_copy(kern_ref.at[pl.ds(c * share, share)], kern, kern_sem)
    fetch.start()
    pl.semaphore_wait(barrier, cols + rows - 2)

    copies = []
    for d in range(1, cols):
        to = lax.rem(c + d, cols)
        copy = pltpu.make_async_remote_copy(
            part_ref.at[to], got1.at[d], send1.at[d], recv1.at[d], device_id=(r, to), device_id_type=MESH)
        copy.start()
        copies.append(copy)
    depth = part_ref.shape[1]
    shape = (rows * freqs, depth)
    rid, rest = split(lax.broadcasted_iota(jnp.int32, shape, 0), freqs)
    fid, sid = split(rest, cols)
    _, fin = split(lax.broadcasted_iota(jnp.int32, shape, 1), share)
    chosen = jnp.where((rid * cols + sid == subs_ref[...]) & (fid == fin), 1.0, 0.0)
    total = part_ref[c]
    for d in range(1, cols):
        copies[d - 1].wait()
        total = total + got1[d]
    spread[...] = jnp.dot(chosen, total, precision=lax.Precision.HIGHEST,
                          preferred_element_type=jnp.float32).reshape(spread.shape)
    copies = []
    for d in range(1, rows):
        to = lax.rem(r + d, rows)
        copy = pltpu.make_async_remote_copy(
            spread.at[to], got2.at[d], send2.at[d], recv2.at[d], device_id=(to, c), device_id_type=MESH)
        copy.start()
        copies.append(copy)
    total = spread[r]
    fetch.wait()
    for d in range(1, rows):
        copies[d - 1].wait()
        total = total + got2[d]
    binned = total.astype(jnp.bfloat16)
    for f in range(share):
        power = jnp.dot(binned[f * cols:(f + 1) * cols], kern[f], preferred_element_type=jnp.float32)
        scale = lax.rsqrt(jnp.mean(power * power, axis=1, keepdims=True) + 1e-06)
        power = power * scale
        for k in range(cols):
            ready[k, f:f + 1, :] = power[k:k + 1]
    copies = []
    for d in range(1, cols):
        to = lax.rem(c + d, cols)
        copy = pltpu.make_async_remote_copy(
            ready.at[to], got3.at[d], send3.at[d], recv3.at[d], device_id=(r, to), device_id_type=MESH)
        copy.start()
        copies.append(copy)
    out_ref[c] = ready[c]
    for d in range(1, cols):
        copies[d - 1].wait()
        out_ref[lax.rem(c - d + cols, cols)] = got3[d]


def finish(partial_value, slot_subs, kernel):
    rows, cols = lax.axis_size("row"), lax.axis_size("col")
    depth = partial_value.shape[1]
    freqs, _, speeds = kernel.shape
    share = freqs // cols
    dma = pltpu.SemaphoreType.DMA
    vmem = pl.BlockSpec(memory_space=pltpu.VMEM)
    return pl.pallas_call(
        finish_kernel,
        out_shape=jax.ShapeDtypeStruct((cols, share, speeds), jnp.float32),
        in_specs=[vmem, vmem, pl.BlockSpec(memory_space=pl.ANY)],
        out_specs=vmem,
        scratch_shapes=[
            pltpu.VMEM((cols, depth, NBIN), jnp.float32),
            pltpu.VMEM((rows, freqs, NBIN), jnp.float32),
            pltpu.VMEM((rows, freqs, NBIN), jnp.float32),
            pltpu.VMEM((cols, share, speeds), jnp.float32),
            pltpu.VMEM((cols, share, speeds), jnp.float32),
            pltpu.VMEM((share, NBIN, speeds), jnp.bfloat16),
            dma, dma((cols,)), dma((cols,)), dma((rows,)), dma((rows,)), dma((cols,)), dma((cols,)),
        ],
        compiler_params=pltpu.CompilerParams(collective_id=1, has_side_effects=True),
        name="finish",
    )(partial_value, jnp.repeat(slot_subs, share)[None], kernel)


def on_device(spectra, pair_bins, row_subs, station_subs, kernel):
    shard, freqs, _ = spectra.shape
    rows, cols = lax.axis_size("row"), lax.axis_size("col")
    r, c = lax.axis_index("row"), lax.axis_index("col")
    row_spectra, col_spectra = gather(spectra.transpose(1, 0, 2))
    slot_subs = row_subs[0]
    slots = slot_subs.shape[0]
    members = station_subs.shape[1]
    row_members = lax.dynamic_slice_in_dim(station_subs, r * cols * shard, cols * shard, 0)
    col_members = lax.dynamic_index_in_dim(
        station_subs.reshape(rows, cols, shard, members), c, 1, keepdims=False).reshape(rows * shard, members)
    row_mask = jnp.any(row_members[:, None, :] == slot_subs[None, :, None], axis=2).astype(jnp.bfloat16)
    col_mask = jnp.any(col_members[None, :, :] == slot_subs[:, None, None], axis=2).astype(jnp.bfloat16)
    row_mask = jnp.broadcast_to(row_mask[:, :, None], (cols * shard, slots, rows * shard))
    partial_value = bin_pairs(row_spectra, col_spectra, pair_bins, row_mask, col_mask)
    return finish(partial_value, slot_subs, kernel).reshape(1, freqs, kernel.shape[2])


def solution(mesh):
    in_specs = (P(("row", "col"), None, None), P("row", "col"), P("row", None), P(), P())
    out_specs = P(("row", "col"), None, None)
    return jax.shard_map(
        on_device, mesh=mesh, in_specs=in_specs, out_specs=out_specs, check_vma=False
    )
```

```python
import functools

import jax
import jax.numpy as jnp
from jax import lax
from jax.experimental import pallas as pl
from jax.experimental.pallas import tpu as pltpu
from jax.sharding import PartitionSpec as P

MESH = pl.DeviceIdType.MESH
NT = (((1,), (1,)), ((), ()))
NBIN = 256
HALVES = 2
PIECES = 4
UNROLL = 8
DIRECT = 2


def split(x, n):
    if n & (n - 1) == 0:
        return x >> (n.bit_length() - 1), x & (n - 1)
    return lax.div(x, n), lax.rem(x, n)


def body(rows, cols, x_ref, bins_ref, subs_ref, members_ref, kern_ref, out_ref,
         xf, xt, rowbuf, colbuf, member, pmask, onehot, cross, w0, w1, acc,
         part, got1, spread, got2, ready, got3, kern,
         own_sem, kern_sem, row_send, row_recv, sib_send, sib_recv, fwd_send, fwd_recv,
         col_send, col_recv, send1, recv1, send2, recv2, send3, recv3):
    r, c = lax.axis_index("row"), lax.axis_index("col")
    shard, freqs, _ = x_ref.shape
    span, width = bins_ref.shape
    slots = subs_ref.shape[1]
    pairs = cols // 2
    g, h = c // 2, c % 2
    sib = g * 2 + (1 - h)
    psize = freqs // PIECES
    half = freqs // HALVES
    share = half // cols
    steps = span // UNROLL
    bf16, f32 = jnp.bfloat16, jnp.float32

    barrier = pltpu.get_barrier_semaphore()
    for d in range(1, cols):
        pl.semaphore_signal(barrier, inc=1, device_id=(r, lax.rem(c + d, cols)), device_id_type=MESH)
    for d in range(1, rows):
        pl.semaphore_signal(barrier, inc=1, device_id=(lax.rem(r + d, rows), c), device_id_type=MESH)
    fetches = []
    for q in range(HALVES):
        fetch = pltpu.make_async_copy(kern_ref.at[pl.ds(q * half + c * share, share)], kern.at[q], kern_sem.at[q])
        fetch.start()
        fetches.append(fetch)
    xf[...] = x_ref[...].astype(f32).reshape(shard * freqs, x_ref.shape[2])
    for f in range(freqs):
        xt[f] = xf[pl.ds(f, shard, stride=freqs), :].astype(bf16)
    pl.semaphore_wait(barrier, cols + rows - 2)

    def slot(ref, index, k):
        return ref.at[pl.ds(k * psize, psize), pl.ds(pl.multiple_of(index * shard, shard), shard), :]

    def row_copy(d, k):
        return pltpu.make_async_remote_copy(
            xt.at[pl.ds(k * psize, psize)], slot(rowbuf, c, k), row_send.at[d, k], row_recv.at[d, k],
            device_id=(r, lax.rem(g + d, pairs) * 2 + h), device_id_type=MESH)

    def sib_copy(k):
        return pltpu.make_async_remote_copy(
            xt.at[pl.ds(k * psize, psize)], slot(rowbuf, c, k), sib_send.at[k], sib_recv.at[k],
            device_id=(r, sib), device_id_type=MESH)

    def fwd_copy(d, k):
        place = slot(rowbuf, lax.rem(g - d + pairs, pairs) * 2 + h, k)
        return pltpu.make_async_remote_copy(
            place, place, fwd_send.at[d, k], fwd_recv.at[d, k], device_id=(r, sib), device_id_type=MESH)

    def col_send_copy(way, d, k):
        if d <= DIRECT:
            return (r + way * d >= 0) & (r + way * d < rows), pltpu.make_async_remote_copy(
                xt.at[pl.ds(k * psize, psize)], slot(colbuf, r, k),
                col_send.at[(way + 1) // 2, d, k], col_recv.at[(way + 1) // 2, d, k],
                device_id=(lax.rem(r + way * d + rows, rows), c), device_id_type=MESH)
        source = lax.rem(r - way * (d - 1) + rows, rows)
        place = slot(colbuf, source, k)
        there = r + way
        back = r - way * (d - 1)
        return (there >= 0) & (there < rows) & (back >= 0) & (back < rows), pltpu.make_async_remote_copy(
            place, place, col_send.at[(way + 1) // 2, d, k], col_recv.at[(way + 1) // 2, d, k],
            device_id=(lax.rem(there + rows, rows), c), device_id_type=MESH)

    def col_wait(way, d, k):
        back = r - way * d

        @pl.when((back >= 0) & (back < rows))
        def _():
            place = slot(colbuf, lax.rem(back + rows, rows), k)
            pltpu.make_async_remote_copy(
                place, place, col_send.at[(way + 1) // 2, d, k], col_recv.at[(way + 1) // 2, d, k],
                device_id=(lax.rem(r + way + rows, rows), c), device_id_type=MESH).wait_recv()

    def start_if(made):
        pl.when(made[0])(made[1].start)

    for k in range(PIECES):
        for d in range(1, min(DIRECT, rows - 1) + 1):
            start_if(col_send_copy(1, d, k))
            start_if(col_send_copy(-1, d, k))
        for d in range(1, pairs):
            row_copy(d, k).start()
        sib_copy(k).start()
    own = [pltpu.make_async_copy(xt, rowbuf.at[:, pl.ds(pl.multiple_of(c * shard, shard), shard), :], own_sem.at[0]),
           pltpu.make_async_copy(xt, colbuf.at[:, pl.ds(pl.multiple_of(r * shard, shard), shard), :], own_sem.at[1])]
    for copy in own:
        copy.start()

    def pass_on(k):
        for d in range(1, pairs):
            row_copy(d, k).wait_recv()
            fwd_copy(d, k).start()
        for d in range(1, rows):
            for way in (1, -1):
                col_wait(way, d, k)
                if d >= DIRECT and d + 1 < rows:
                    start_if(col_send_copy(way, d + 1, k))

    def rest(k):
        sib_copy(k).wait_recv()
        for d in range(1, pairs):
            fwd_copy(d, k).wait_recv()

    stations = members_ref.shape[1]
    sub_at = lax.broadcasted_iota(jnp.int32, (slots, stations), 0)
    slot_ids = jnp.zeros((slots, stations), jnp.int32)
    for s in range(slots):
        slot_ids = jnp.where(sub_at == s, subs_ref[0, s], slot_ids)
    found = jnp.zeros((slots, stations), f32)
    for m in range(members_ref.shape[0]):
        found = jnp.where(slot_ids == members_ref[m:m + 1, :], 1.0, found)
    member[...] = found
    name = lax.broadcasted_iota(jnp.int32, (stations, width), 0)
    block_id, inside = split(lax.broadcasted_iota(jnp.int32, (stations, width), 1), shard)
    picked = jnp.where(name == (block_id * cols + c) * shard + inside, 1.0, 0.0).astype(bf16)
    col_mask = jnp.dot(found.astype(bf16), picked, preferred_element_type=f32)
    lane = lax.broadcasted_iota(jnp.int32, (slots, span), 1)
    row_mask = member[:, pl.ds(pl.multiple_of(r * span, span), span)]

    def prepare(first, last):
        def one(step, carry):
            for u in range(UNROLL):
                i = step * UNROLL + u
                hit = jnp.sum(jnp.where(lane == i, row_mask, 0.0), axis=1, keepdims=True)
                pmask[i] = (hit * col_mask).astype(bf16)
                ids = lax.broadcasted_iota(jnp.int32, (NBIN, width), 0)
                onehot[step, :, u * width:(u + 1) * width] = jnp.where(
                    ids == bins_ref[pl.ds(i, 1), :], 1.0, 0.0).astype(bf16)
            return carry
        lax.fori_loop(first, last, one, 0)

    def correlate(q):
        def one(f, carry):
            cross[pl.ds(f, span, stride=freqs), :] = lax.dot_general(
                rowbuf[f], colbuf[f], NT, preferred_element_type=f32)
            return carry
        lax.fori_loop(q * half, (q + 1) * half, one, 0, unroll=4)

    def build(q, step, w):
        for u in range(UNROLL):
            i = step * UNROLL + u
            block = cross[pl.ds(pl.multiple_of(i * freqs + q * half, half), half), :].astype(bf16)
            weighted = pmask[i][:, None, :] * block[None]
            w[:, u * width:(u + 1) * width] = weighted.reshape(slots * half, width)

    def multiply(step, w):
        acc[...] += lax.dot_general(w[...], onehot[step], NT, preferred_element_type=f32)

    def accumulate(q, first, last):
        def two(pair, carry):
            build(q, 2 * pair + 1, w1)
            multiply(2 * pair, w0)
            build(q, lax.min(2 * pair + 2, steps - 1), w0)
            multiply(2 * pair + 1, w1)
            return carry
        lax.fori_loop(first, last, two, 0)

    def copy1(q, d):
        to = lax.rem(c + d, cols)
        return pltpu.make_async_remote_copy(
            part.at[q, to], got1.at[q, d], send1.at[q, d], recv1.at[q, d], device_id=(r, to), device_id_type=MESH)

    def hand_out(q):
        for k in range(cols):
            for s in range(slots):
                part[q, k, s * share:(s + 1) * share, :] = acc[s * half + k * share:s * half + (k + 1) * share, :]
        for d in range(1, cols):
            copy1(q, d).start()

    quarter = steps // 4
    per_half = PIECES // HALVES
    prepare(0, quarter * 2)
    pass_on(0)
    prepare(quarter * 2, quarter * 3)
    pass_on(1)
    prepare(quarter * 3, steps)
    for copy in own:
        copy.wait()
    for k in range(per_half):
        rest(k)
    correlate(0)
    acc[...] = jnp.zeros_like(acc)
    build(0, 0, w0)
    accumulate(0, 0, steps // 4)
    pass_on(2)
    accumulate(0, steps // 4, steps // 2)
    hand_out(0)
    pass_on(3)
    for k in range(per_half, PIECES):
        rest(k)
    correlate(1)
    acc[...] = jnp.zeros_like(acc)
    build(1, 0, w0)
    accumulate(1, 0, steps // 2)
    hand_out(1)

    depth = slots * share
    shape = (rows * share * cols, depth)
    rid, tail = split(lax.broadcasted_iota(jnp.int32, shape, 0), share * cols)
    fid, sid = split(tail, cols)
    place, fin = split(lax.broadcasted_iota(jnp.int32, shape, 1), share)
    listed = jnp.zeros(shape, jnp.int32)
    for s in range(slots):
        listed = jnp.where(place == s, subs_ref[0, s], listed)
    chosen = jnp.where((rid * cols + sid == listed) & (fid == fin), 1.0, 0.0)

    def copy2(q, d):
        to = lax.rem(r + d, rows)
        return pltpu.make_async_remote_copy(
            spread.at[q, to], got2.at[q, d], send2.at[q, d], recv2.at[q, d], device_id=(to, c), device_id_type=MESH)

    for q in range(HALVES):
        total = part[q, c]
        for d in range(1, cols):
            copy1(q, d).wait()
            total = total + got1[q, d]
        spread[q] = jnp.dot(chosen, total, precision=lax.Precision.HIGHEST,
                            preferred_element_type=f32).reshape(rows, share * cols, NBIN)
        for d in range(1, rows):
            copy2(q, d).start()
    for q in range(HALVES):
        fetches[q].wait()
        total = spread[q, r]
        for d in range(1, rows):
            copy2(q, d).wait()
            total = total + got2[q, d]
        binned = total.astype(bf16)
        for f in range(share):
            power = jnp.dot(binned[f * cols:(f + 1) * cols], kern[q, f], preferred_element_type=f32)
            power = power * lax.rsqrt(jnp.mean(power * power, axis=1, keepdims=True) + 1e-06)
            for k in range(cols):
                ready[k, q * share + f:q * share + f + 1, :] = power[k:k + 1]

    def copy3(d):
        to = lax.rem(c + d, cols)
        return pltpu.make_async_remote_copy(
            ready.at[to], got3.at[d], send3.at[d], recv3.at[d], device_id=(r, to), device_id_type=MESH)

    def put(source, block):
        for q in range(HALVES):
            for f in range(share):
                out_ref[0, pl.ds(q * half + source * share + f, 1), :] = block[q * share + f:q * share + f + 1]

    for d in range(1, cols):
        copy3(d).start()
    put(c, ready[c])
    for d in range(1, cols):
        copy3(d).wait()
        put(lax.rem(c - d + cols, cols), got3[d])
    for k in range(PIECES):
        sib_copy(k).wait_send()
        for d in range(1, pairs):
            row_copy(d, k).wait_send()
            fwd_copy(d, k).wait_send()
        for d in range(1, rows):
            for way in (1, -1):
                made = col_send_copy(way, d, k)
                pl.when(made[0])(made[1].wait_send)


def on_device(spectra, pair_bins, row_subs, station_subs, kernel):
    shard, freqs, width = spectra.shape
    rows, cols = lax.axis_size("row"), lax.axis_size("col")
    span, group = pair_bins.shape
    slots = row_subs.shape[1]
    half = freqs // HALVES
    share = half // cols
    depth = slots * share
    speeds = kernel.shape[2]
    pairs = cols // 2
    dma = pltpu.SemaphoreType.DMA
    vmem = pl.BlockSpec(memory_space=pltpu.VMEM)
    bf16, f32 = jnp.bfloat16, jnp.float32
    return pl.pallas_call(
        functools.partial(body, rows, cols),
        out_shape=jax.ShapeDtypeStruct((1, freqs, speeds), f32),
        in_specs=[vmem, vmem, pl.BlockSpec(memory_space=pltpu.SMEM), vmem, pl.BlockSpec(memory_space=pl.ANY)],
        out_specs=vmem,
        scratch_shapes=[
            pltpu.VMEM((shard * freqs, width), f32),
            pltpu.VMEM((freqs, shard, width), bf16),
            pltpu.VMEM((freqs, cols * shard, width), bf16),
            pltpu.VMEM((freqs, rows * shard, width), bf16),
            pltpu.VMEM((slots, station_subs.shape[0]), f32),
            pltpu.VMEM((span, slots, group), bf16),
            pltpu.VMEM((span // UNROLL, NBIN, UNROLL * group), bf16),
            pltpu.VMEM((span * freqs, group), f32),
            pltpu.VMEM((slots * half, UNROLL * group), bf16),
            pltpu.VMEM((slots * half, UNROLL * group), bf16),
            pltpu.VMEM((slots * half, NBIN), f32),
            pltpu.VMEM((HALVES, cols, depth, NBIN), f32),
            pltpu.VMEM((HALVES, cols, depth, NBIN), f32),
            pltpu.VMEM((HALVES, rows, share * cols, NBIN), f32),
            pltpu.VMEM((HALVES, rows, share * cols, NBIN), f32),
            pltpu.VMEM((cols, HALVES * share, speeds), f32),
            pltpu.VMEM((cols, HALVES * share, speeds), f32),
            pltpu.VMEM((HALVES, share, NBIN, speeds), bf16),
            dma((2,)), dma((HALVES,)),
            dma((pairs, PIECES)), dma((pairs, PIECES)), dma((PIECES,)), dma((PIECES,)),
            dma((pairs, PIECES)), dma((pairs, PIECES)),
            dma((2, rows, PIECES)), dma((2, rows, PIECES)),
            dma((HALVES, cols)), dma((HALVES, cols)), dma((HALVES, rows)), dma((HALVES, rows)),
            dma((cols,)), dma((cols,)),
        ],
        compiler_params=pltpu.CompilerParams(collective_id=0, has_side_effects=True, vmem_limit_bytes=62 << 20),
        name="dispersion",
    )(spectra, pair_bins, row_subs, station_subs.T, kernel)


def solution(mesh):
    in_specs = (P(("row", "col"), None, None), P("row", "col"), P("row", None), P(), P())
    out_specs = P(("row", "col"), None, None)
    return jax.shard_map(
        on_device, mesh=mesh, in_specs=in_specs, out_specs=out_specs, check_vma=False
    )
```

```python
import functools

import jax
import jax.numpy as jnp
from jax import lax
from jax.experimental import pallas as pl
from jax.experimental.pallas import tpu as pltpu
from jax.sharding import PartitionSpec as P

MESH = pl.DeviceIdType.MESH
NT = (((1,), (1,)), ((), ()))
NBIN = 256
HALVES = 2
PIECES = 4
UNROLL = 8
DIRECT = 2


def split(x, n):
    if n & (n - 1) == 0:
        return x >> (n.bit_length() - 1), x & (n - 1)
    return lax.div(x, n), lax.rem(x, n)


def body(rows, cols, x_ref, bins_ref, subs_ref, members_ref, kern_ref, out_ref,
         xf, xt, rowbuf, colbuf, member, pmask, onehot, cross, w0, w1, acc,
         part, got1, spread, got2, ready, got3, kern,
         own_sem, kern_sem, row_send, row_recv, sib_send, sib_recv, fwd_send, fwd_recv,
         col_send, col_recv, send1, recv1, send2, recv2, send3, recv3):
    r, c = lax.axis_index("row"), lax.axis_index("col")
    shard, freqs, _ = x_ref.shape
    span, width = bins_ref.shape
    slots = subs_ref.shape[1]
    pairs = cols // 2
    g, h = c // 2, c % 2
    sib = g * 2 + (1 - h)
    psize = freqs // PIECES
    half = freqs // HALVES
    share = half // cols
    steps = span // UNROLL
    bf16, f32 = jnp.bfloat16, jnp.float32

    barrier = pltpu.get_barrier_semaphore()
    for d in range(1, cols):
        pl.semaphore_signal(barrier, inc=1, device_id=(r, lax.rem(c + d, cols)), device_id_type=MESH)
    for d in range(1, rows):
        pl.semaphore_signal(barrier, inc=1, device_id=(lax.rem(r + d, rows), c), device_id_type=MESH)
    fetches = []
    for q in range(HALVES):
        fetch = pltpu.make_async_copy(kern_ref.at[pl.ds(q * half + c * share, share)], kern.at[q], kern_sem.at[q])
        fetch.start()
        fetches.append(fetch)
    xf[...] = x_ref[...].astype(f32).reshape(shard * freqs, x_ref.shape[2])
    for f in range(freqs):
        xt[f] = xf[pl.ds(f, shard, stride=freqs), :].astype(bf16)
    pl.semaphore_wait(barrier, cols + rows - 2)

    def slot(ref, index, k):
        return ref.at[pl.ds(k * psize, psize), pl.ds(pl.multiple_of(index * shard, shard), shard), :]

    def row_copy(d, k):
        return pltpu.make_async_remote_copy(
            xt.at[pl.ds(k * psize, psize)], slot(rowbuf, c, k), row_send.at[d, k], row_recv.at[d, k],
            device_id=(r, lax.rem(g + d, pairs) * 2 + h), device_id_type=MESH)

    def sib_copy(k):
        return pltpu.make_async_remote_copy(
            xt.at[pl.ds(k * psize, psize)], slot(rowbuf, c, k), sib_send.at[k], sib_recv.at[k],
            device_id=(r, sib), device_id_type=MESH)

    def fwd_copy(d, k):
        place = slot(rowbuf, lax.rem(g - d + pairs, pairs) * 2 + h, k)
        return pltpu.make_async_remote_copy(
            place, place, fwd_send.at[d, k], fwd_recv.at[d, k], device_id=(r, sib), device_id_type=MESH)

    def col_send_copy(way, d, k):
        if d <= DIRECT:
            return (r + way * d >= 0) & (r + way * d < rows), pltpu.make_async_remote_copy(
                xt.at[pl.ds(k * psize, psize)], slot(colbuf, r, k),
                col_send.at[(way + 1) // 2, d, k], col_recv.at[(way + 1) // 2, d, k],
                device_id=(lax.rem(r + way * d + rows, rows), c), device_id_type=MESH)
        source = lax.rem(r - way * (d - 1) + rows, rows)
        place = slot(colbuf, source, k)
        there = r + way
        back = r - way * (d - 1)
        return (there >= 0) & (there < rows) & (back >= 0) & (back < rows), pltpu.make_async_remote_copy(
            place, place, col_send.at[(way + 1) // 2, d, k], col_recv.at[(way + 1) // 2, d, k],
            device_id=(lax.rem(there + rows, rows), c), device_id_type=MESH)

    def col_wait(way, d, k):
        back = r - way * d

        @pl.when((back >= 0) & (back < rows))
        def _():
            place = slot(colbuf, lax.rem(back + rows, rows), k)
            pltpu.make_async_remote_copy(
                place, place, col_send.at[(way + 1) // 2, d, k], col_recv.at[(way + 1) // 2, d, k],
                device_id=(lax.rem(r + way + rows, rows), c), device_id_type=MESH).wait_recv()

    def start_if(made):
        pl.when(made[0])(made[1].start)

    def send(k):
        for d in range(1, min(DIRECT, rows - 1) + 1):
            start_if(col_send_copy(1, d, k))
            start_if(col_send_copy(-1, d, k))
        for d in range(1, pairs):
            row_copy(d, k).start()
        sib_copy(k).start()

    per_half = PIECES // HALVES
    for k in range(per_half):
        send(k)
    own = [pltpu.make_async_copy(xt, rowbuf.at[:, pl.ds(pl.multiple_of(c * shard, shard), shard), :], own_sem.at[0]),
           pltpu.make_async_copy(xt, colbuf.at[:, pl.ds(pl.multiple_of(r * shard, shard), shard), :], own_sem.at[1])]
    for copy in own:
        copy.start()

    def pass_on(k):
        for d in range(1, pairs):
            row_copy(d, k).wait_recv()
            fwd_copy(d, k).start()
        for d in range(1, rows):
            for way in (1, -1):
                col_wait(way, d, k)
                if d >= DIRECT and d + 1 < rows:
                    start_if(col_send_copy(way, d + 1, k))

    def rest(k):
        sib_copy(k).wait_recv()
        for d in range(1, pairs):
            fwd_copy(d, k).wait_recv()

    stations = members_ref.shape[1]
    sub_at = lax.broadcasted_iota(jnp.int32, (slots, stations), 0)
    slot_ids = jnp.zeros((slots, stations), jnp.int32)
    for s in range(slots):
        slot_ids = jnp.where(sub_at == s, subs_ref[0, s], slot_ids)
    found = jnp.zeros((slots, stations), f32)
    for m in range(members_ref.shape[0]):
        found = jnp.where(slot_ids == members_ref[m:m + 1, :], 1.0, found)
    member[...] = found
    name = lax.broadcasted_iota(jnp.int32, (stations, width), 0)
    block_id, inside = split(lax.broadcasted_iota(jnp.int32, (stations, width), 1), shard)
    picked = jnp.where(name == (block_id * cols + c) * shard + inside, 1.0, 0.0).astype(bf16)
    col_mask = jnp.dot(found.astype(bf16), picked, preferred_element_type=f32)
    lane = lax.broadcasted_iota(jnp.int32, (slots, span), 1)
    row_mask = member[:, pl.ds(pl.multiple_of(r * span, span), span)]

    def prepare(first, last):
        def one(step, carry):
            for u in range(UNROLL):
                i = step * UNROLL + u
                hit = jnp.sum(jnp.where(lane == i, row_mask, 0.0), axis=1, keepdims=True)
                pmask[i] = (hit * col_mask).astype(bf16)
                ids = lax.broadcasted_iota(jnp.int32, (NBIN, width), 0)
                onehot[step, :, u * width:(u + 1) * width] = jnp.where(
                    ids == bins_ref[pl.ds(i, 1), :], 1.0, 0.0).astype(bf16)
            return carry
        lax.fori_loop(first, last, one, 0)

    def correlate(q):
        def one(f, carry):
            cross[pl.ds(f, span, stride=freqs), :] = lax.dot_general(
                rowbuf[f], colbuf[f], NT, preferred_element_type=f32)
            return carry
        lax.fori_loop(q * half, (q + 1) * half, one, 0, unroll=4)

    def build(q, step, w):
        for u in range(UNROLL):
            i = step * UNROLL + u
            block = cross[pl.ds(pl.multiple_of(i * freqs + q * half, half), half), :].astype(bf16)
            weighted = pmask[i][:, None, :] * block[None]
            w[:, u * width:(u + 1) * width] = weighted.reshape(slots * half, width)

    def multiply(step, w):
        acc[...] += lax.dot_general(w[...], onehot[step], NT, preferred_element_type=f32)

    def accumulate(q, first, last):
        def two(pair, carry):
            build(q, 2 * pair + 1, w1)
            multiply(2 * pair, w0)
            build(q, lax.min(2 * pair + 2, steps - 1), w0)
            multiply(2 * pair + 1, w1)
            return carry
        lax.fori_loop(first, last, two, 0)

    def copy1(q, d):
        to = lax.rem(c + d, cols)
        return pltpu.make_async_remote_copy(
            part.at[q, to], got1.at[q, d], send1.at[q, d], recv1.at[q, d], device_id=(r, to), device_id_type=MESH)

    def hand_out(q):
        for k in range(cols):
            for s in range(slots):
                part[q, k, s * share:(s + 1) * share, :] = acc[s * half + k * share:s * half + (k + 1) * share, :]
        for d in range(1, cols):
            copy1(q, d).start()

    depth = slots * share
    shape = (rows * share * cols, depth)
    rid, tail = split(lax.broadcasted_iota(jnp.int32, shape, 0), share * cols)
    fid, sid = split(tail, cols)
    place, fin = split(lax.broadcasted_iota(jnp.int32, shape, 1), share)
    listed = jnp.zeros(shape, jnp.int32)
    for s in range(slots):
        listed = jnp.where(place == s, subs_ref[0, s], listed)
    chosen = jnp.where((rid * cols + sid == listed) & (fid == fin), 1.0, 0.0)

    def copy2(q, d):
        to = lax.rem(r + d, rows)
        return pltpu.make_async_remote_copy(
            spread.at[q, to], got2.at[q, d], send2.at[q, d], recv2.at[q, d], device_id=(to, c), device_id_type=MESH)

    def to_owners(q):
        total = part[q, c]
        for d in range(1, cols):
            copy1(q, d).wait()
            total = total + got1[q, d]
        spread[q] = jnp.dot(chosen, total, precision=lax.Precision.HIGHEST,
                            preferred_element_type=f32).reshape(rows, share * cols, NBIN)
        for d in range(1, rows):
            copy2(q, d).start()

    quarter = steps // 4
    prepare(0, quarter * 2)
    pass_on(0)
    send(2)
    prepare(quarter * 2, quarter * 3)
    pass_on(1)
    send(3)
    prepare(quarter * 3, steps)
    for copy in own:
        copy.wait()
    for k in range(per_half):
        rest(k)
    correlate(0)
    acc[...] = jnp.zeros_like(acc)
    build(0, 0, w0)
    accumulate(0, 0, steps // 4)
    pass_on(2)
    accumulate(0, steps // 4, steps // 2)
    hand_out(0)
    pass_on(3)
    for k in range(per_half, PIECES):
        rest(k)
    correlate(1)
    acc[...] = jnp.zeros_like(acc)
    build(1, 0, w0)
    accumulate(1, 0, steps // 4)
    to_owners(0)
    accumulate(1, steps // 4, steps // 2)
    hand_out(1)
    to_owners(1)

    for q in range(HALVES):
        fetches[q].wait()
        total = spread[q, r]
        for d in range(1, rows):
            copy2(q, d).wait()
            total = total + got2[q, d]
        binned = total.astype(bf16)
        for f in range(share):
            power = jnp.dot(binned[f * cols:(f + 1) * cols], kern[q, f], preferred_element_type=f32)
            power = power * lax.rsqrt(jnp.mean(power * power, axis=1, keepdims=True) + 1e-06)
            for k in range(cols):
                ready[k, q * share + f:q * share + f + 1, :] = power[k:k + 1]

    def copy3(d):
        to = lax.rem(c + d, cols)
        return pltpu.make_async_remote_copy(
            ready.at[to], got3.at[d], send3.at[d], recv3.at[d], device_id=(r, to), device_id_type=MESH)

    def put(source, block):
        for q in range(HALVES):
            for f in range(share):
                out_ref[0, pl.ds(q * half + source * share + f, 1), :] = block[q * share + f:q * share + f + 1]

    for d in range(1, cols):
        copy3(d).start()
    put(c, ready[c])
    for d in range(1, cols):
        copy3(d).wait()
        put(lax.rem(c - d + cols, cols), got3[d])
    for k in range(PIECES):
        sib_copy(k).wait_send()
        for d in range(1, pairs):
            row_copy(d, k).wait_send()
            fwd_copy(d, k).wait_send()
        for d in range(1, rows):
            for way in (1, -1):
                made = col_send_copy(way, d, k)
                pl.when(made[0])(made[1].wait_send)


def on_device(spectra, pair_bins, row_subs, station_subs, kernel):
    shard, freqs, width = spectra.shape
    rows, cols = lax.axis_size("row"), lax.axis_size("col")
    span, group = pair_bins.shape
    slots = row_subs.shape[1]
    half = freqs // HALVES
    share = half // cols
    depth = slots * share
    speeds = kernel.shape[2]
    pairs = cols // 2
    dma = pltpu.SemaphoreType.DMA
    vmem = pl.BlockSpec(memory_space=pltpu.VMEM)
    bf16, f32 = jnp.bfloat16, jnp.float32
    return pl.pallas_call(
        functools.partial(body, rows, cols),
        out_shape=jax.ShapeDtypeStruct((1, freqs, speeds), f32),
        in_specs=[vmem, vmem, pl.BlockSpec(memory_space=pltpu.SMEM), vmem, pl.BlockSpec(memory_space=pl.ANY)],
        out_specs=vmem,
        scratch_shapes=[
            pltpu.VMEM((shard * freqs, width), f32),
            pltpu.VMEM((freqs, shard, width), bf16),
            pltpu.VMEM((freqs, cols * shard, width), bf16),
            pltpu.VMEM((freqs, rows * shard, width), bf16),
            pltpu.VMEM((slots, station_subs.shape[0]), f32),
            pltpu.VMEM((span, slots, group), bf16),
            pltpu.VMEM((span // UNROLL, NBIN, UNROLL * group), bf16),
            pltpu.VMEM((span * freqs, group), f32),
            pltpu.VMEM((slots * half, UNROLL * group), bf16),
            pltpu.VMEM((slots * half, UNROLL * group), bf16),
            pltpu.VMEM((slots * half, NBIN), f32),
            pltpu.VMEM((HALVES, cols, depth, NBIN), f32),
            pltpu.VMEM((HALVES, cols, depth, NBIN), f32),
            pltpu.VMEM((HALVES, rows, share * cols, NBIN), f32),
            pltpu.VMEM((HALVES, rows, share * cols, NBIN), f32),
            pltpu.VMEM((cols, HALVES * share, speeds), f32),
            pltpu.VMEM((cols, HALVES * share, speeds), f32),
            pltpu.VMEM((HALVES, share, NBIN, speeds), bf16),
            dma((2,)), dma((HALVES,)),
            dma((pairs, PIECES)), dma((pairs, PIECES)), dma((PIECES,)), dma((PIECES,)),
            dma((pairs, PIECES)), dma((pairs, PIECES)),
            dma((2, rows, PIECES)), dma((2, rows, PIECES)),
            dma((HALVES, cols)), dma((HALVES, cols)), dma((HALVES, rows)), dma((HALVES, rows)),
            dma((cols,)), dma((cols,)),
        ],
        compiler_params=pltpu.CompilerParams(collective_id=0, has_side_effects=True, vmem_limit_bytes=62 << 20),
        name="dispersion",
    )(spectra, pair_bins, row_subs, station_subs.T, kernel)


def solution(mesh):
    in_specs = (P(("row", "col"), None, None), P("row", "col"), P("row", None), P(), P())
    out_specs = P(("row", "col"), None, None)
    return jax.shard_map(
        on_device, mesh=mesh, in_specs=in_specs, out_specs=out_specs, check_vma=False
    )
```

```python
import functools

import jax
import jax.numpy as jnp
from jax import lax
from jax.experimental import pallas as pl
from jax.experimental.pallas import tpu as pltpu
from jax.sharding import PartitionSpec as P

MESH = pl.DeviceIdType.MESH
NT = (((1,), (1,)), ((), ()))
NBIN = 256
HALVES = 2
PIECES = 4
UNROLL = 8
DIRECT = 2


def split(x, n):
    if n & (n - 1) == 0:
        return x >> (n.bit_length() - 1), x & (n - 1)
    return lax.div(x, n), lax.rem(x, n)


def body(rows, cols, x_ref, bins_ref, subs_ref, members_ref, kern_ref, out_ref,
         xf, xt, rowbuf, colbuf, member, pmask, onehot, cross, w0, w1, acc,
         part, got1, spread, got2, ready, got3, kern,
         own_sem, kern_sem, row_send, row_recv, sib_send, sib_recv, fwd_send, fwd_recv,
         col_send, col_recv, send1, recv1, send2, recv2, send3, recv3):
    r, c = lax.axis_index("row"), lax.axis_index("col")
    shard, freqs, _ = x_ref.shape
    span, width = bins_ref.shape
    slots = subs_ref.shape[1]
    pairs = cols // 2
    g, h = c // 2, c % 2
    sib = g * 2 + (1 - h)
    psize = freqs // PIECES
    half = freqs // HALVES
    share = half // cols
    steps = span // UNROLL
    per_half = PIECES // HALVES
    bf16, f32 = jnp.bfloat16, jnp.float32

    barrier = pltpu.get_barrier_semaphore()
    for d in range(1, cols):
        pl.semaphore_signal(barrier, inc=1, device_id=(r, lax.rem(c + d, cols)), device_id_type=MESH)
    for d in range(1, rows):
        pl.semaphore_signal(barrier, inc=1, device_id=(lax.rem(r + d, rows), c), device_id_type=MESH)
    fetches = []
    for q in range(HALVES):
        fetch = pltpu.make_async_copy(kern_ref.at[pl.ds(q * half + c * share, share)], kern.at[q], kern_sem.at[q])
        fetch.start()
        fetches.append(fetch)
    xf[...] = x_ref[...].astype(f32).reshape(shard * freqs, x_ref.shape[2])
    for f in range(freqs):
        xt[f] = xf[pl.ds(f, shard, stride=freqs), :].astype(bf16)
    pl.semaphore_wait(barrier, cols + rows - 2)

    def slot(ref, index, k):
        return ref.at[pl.ds(k * psize, psize), pl.ds(pl.multiple_of(index * shard, shard), shard), :]

    def row_copy(d, k):
        return pltpu.make_async_remote_copy(
            xt.at[pl.ds(k * psize, psize)], slot(rowbuf, c, k), row_send.at[d, k], row_recv.at[d, k],
            device_id=(r, lax.rem(g + d, pairs) * 2 + h), device_id_type=MESH)

    def sib_copy(k):
        return pltpu.make_async_remote_copy(
            xt.at[pl.ds(k * psize, psize)], slot(rowbuf, c, k), sib_send.at[k], sib_recv.at[k],
            device_id=(r, sib), device_id_type=MESH)

    def fwd_copy(d, k):
        if k >= per_half:
            return pltpu.make_async_remote_copy(
                xt.at[pl.ds(k * psize, psize)], slot(rowbuf, c, k), fwd_send.at[d, k], fwd_recv.at[d, k],
                device_id=(r, lax.rem(g + d, pairs) * 2 + (1 - h)), device_id_type=MESH)
        place = slot(rowbuf, lax.rem(g - d + pairs, pairs) * 2 + h, k)
        return pltpu.make_async_remote_copy(
            place, place, fwd_send.at[d, k], fwd_recv.at[d, k], device_id=(r, sib), device_id_type=MESH)

    def col_send_copy(way, d, k):
        if d <= DIRECT or k >= per_half:
            return (r + way * d >= 0) & (r + way * d < rows), pltpu.make_async_remote_copy(
                xt.at[pl.ds(k * psize, psize)], slot(colbuf, r, k),
                col_send.at[(way + 1) // 2, d, k], col_recv.at[(way + 1) // 2, d, k],
                device_id=(lax.rem(r + way * d + rows, rows), c), device_id_type=MESH)
        source = lax.rem(r - way * (d - 1) + rows, rows)
        place = slot(colbuf, source, k)
        there = r + way
        back = r - way * (d - 1)
        return (there >= 0) & (there < rows) & (back >= 0) & (back < rows), pltpu.make_async_remote_copy(
            place, place, col_send.at[(way + 1) // 2, d, k], col_recv.at[(way + 1) // 2, d, k],
            device_id=(lax.rem(there + rows, rows), c), device_id_type=MESH)

    def col_wait(way, d, k):
        back = r - way * d

        @pl.when((back >= 0) & (back < rows))
        def _():
            place = slot(colbuf, lax.rem(back + rows, rows), k)
            pltpu.make_async_remote_copy(
                place, place, col_send.at[(way + 1) // 2, d, k], col_recv.at[(way + 1) // 2, d, k],
                device_id=(lax.rem(r + way + rows, rows), c), device_id_type=MESH).wait_recv()

    def start_if(made):
        pl.when(made[0])(made[1].start)

    def send(k):
        for d in range(1, (min(DIRECT, rows - 1) if k < per_half else rows - 1) + 1):
            start_if(col_send_copy(1, d, k))
            start_if(col_send_copy(-1, d, k))
        for d in range(1, pairs):
            row_copy(d, k).start()
            if k >= per_half:
                fwd_copy(d, k).start()
        sib_copy(k).start()

    for k in range(per_half):
        send(k)
    own = [pltpu.make_async_copy(xt, rowbuf.at[:, pl.ds(pl.multiple_of(c * shard, shard), shard), :], own_sem.at[0]),
           pltpu.make_async_copy(xt, colbuf.at[:, pl.ds(pl.multiple_of(r * shard, shard), shard), :], own_sem.at[1])]
    for copy in own:
        copy.start()

    def pass_on(k):
        for d in range(1, pairs):
            row_copy(d, k).wait_recv()
            fwd_copy(d, k).start()
        for d in range(1, rows - 1):
            for way in (1, -1):
                col_wait(way, d, k)
                if d >= DIRECT:
                    start_if(col_send_copy(way, d + 1, k))

    def rest(k):
        if k >= per_half:
            for d in range(1, pairs):
                row_copy(d, k).wait_recv()
        for d in range(1 if k >= per_half else rows - 1, rows):
            for way in (1, -1):
                col_wait(way, d, k)
        sib_copy(k).wait_recv()
        for d in range(1, pairs):
            fwd_copy(d, k).wait_recv()

    stations = members_ref.shape[1]
    sub_at = lax.broadcasted_iota(jnp.int32, (slots, stations), 0)
    slot_ids = jnp.zeros((slots, stations), jnp.int32)
    for s in range(slots):
        slot_ids = jnp.where(sub_at == s, subs_ref[0, s], slot_ids)
    found = jnp.zeros((slots, stations), f32)
    for m in range(members_ref.shape[0]):
        found = jnp.where(slot_ids == members_ref[m:m + 1, :], 1.0, found)
    member[...] = found
    name = lax.broadcasted_iota(jnp.int32, (stations, width), 0)
    block_id, inside = split(lax.broadcasted_iota(jnp.int32, (stations, width), 1), shard)
    picked = jnp.where(name == (block_id * cols + c) * shard + inside, 1.0, 0.0).astype(bf16)
    col_mask = jnp.dot(found.astype(bf16), picked, preferred_element_type=f32)
    lane = lax.broadcasted_iota(jnp.int32, (slots, span), 1)
    row_mask = member[:, pl.ds(pl.multiple_of(r * span, span), span)]

    def prepare(first, last):
        def one(step, carry):
            for u in range(UNROLL):
                i = step * UNROLL + u
                hit = jnp.sum(jnp.where(lane == i, row_mask, 0.0), axis=1, keepdims=True)
                pmask[i] = (hit * col_mask).astype(bf16)
                ids = lax.broadcasted_iota(jnp.int32, (NBIN, width), 0)
                onehot[step, :, u * width:(u + 1) * width] = jnp.where(
                    ids == bins_ref[pl.ds(i, 1), :], 1.0, 0.0).astype(bf16)
            return carry
        lax.fori_loop(first, last, one, 0)

    def correlate(q):
        def one(f, carry):
            cross[pl.ds(f, span, stride=freqs), :] = lax.dot_general(
                rowbuf[f], colbuf[f], NT, preferred_element_type=f32)
            return carry
        lax.fori_loop(q * half, (q + 1) * half, one, 0, unroll=4)

    def build(q, step, w):
        for u in range(UNROLL):
            i = step * UNROLL + u
            block = cross[pl.ds(pl.multiple_of(i * freqs + q * half, half), half), :].astype(bf16)
            weighted = pmask[i][:, None, :] * block[None]
            w[:, u * width:(u + 1) * width] = weighted.reshape(slots * half, width)

    def multiply(step, w):
        acc[...] += lax.dot_general(w[...], onehot[step], NT, preferred_element_type=f32)

    def accumulate(q, first, last):
        def two(pair, carry):
            build(q, 2 * pair + 1, w1)
            multiply(2 * pair, w0)
            build(q, lax.min(2 * pair + 2, steps - 1), w0)
            multiply(2 * pair + 1, w1)
            return carry
        lax.fori_loop(first, last, two, 0)

    def copy1(q, d):
        to = lax.rem(c + d, cols)
        return pltpu.make_async_remote_copy(
            part.at[q, to], got1.at[q, d], send1.at[q, d], recv1.at[q, d], device_id=(r, to), device_id_type=MESH)

    def hand_out(q):
        for k in range(cols):
            for s in range(slots):
                part[q, k, s * share:(s + 1) * share, :] = acc[s * half + k * share:s * half + (k + 1) * share, :]
        for d in range(1, cols):
            copy1(q, d).start()

    depth = slots * share
    shape = (rows * share * cols, depth)
    rid, tail = split(lax.broadcasted_iota(jnp.int32, shape, 0), share * cols)
    fid, sid = split(tail, cols)
    place, fin = split(lax.broadcasted_iota(jnp.int32, shape, 1), share)
    listed = jnp.zeros(shape, jnp.int32)
    for s in range(slots):
        listed = jnp.where(place == s, subs_ref[0, s], listed)
    chosen = jnp.where((rid * cols + sid == listed) & (fid == fin), 1.0, 0.0)

    def copy2(q, d):
        to = lax.rem(r + d, rows)
        return pltpu.make_async_remote_copy(
            spread.at[q, to], got2.at[q, d], send2.at[q, d], recv2.at[q, d], device_id=(to, c), device_id_type=MESH)

    def to_owners(q):
        total = part[q, c]
        for d in range(1, cols):
            copy1(q, d).wait()
            total = total + got1[q, d]
        spread[q] = jnp.dot(chosen, total, precision=lax.Precision.HIGHEST,
                            preferred_element_type=f32).reshape(rows, share * cols, NBIN)
        for d in range(1, rows):
            copy2(q, d).start()

    prepare(0, steps // 2)
    for k in range(per_half):
        pass_on(k)
    for k in range(per_half, PIECES):
        send(k)
    prepare(steps // 2, steps)
    for copy in own:
        copy.wait()
    for k in range(per_half):
        rest(k)
    correlate(0)
    acc[...] = jnp.zeros_like(acc)
    build(0, 0, w0)
    accumulate(0, 0, steps // 2)
    hand_out(0)
    for k in range(per_half, PIECES):
        rest(k)
    correlate(1)
    acc[...] = jnp.zeros_like(acc)
    build(1, 0, w0)
    accumulate(1, 0, steps // 4)
    to_owners(0)
    accumulate(1, steps // 4, steps // 2)
    hand_out(1)
    to_owners(1)

    for q in range(HALVES):
        fetches[q].wait()
        total = spread[q, r]
        for d in range(1, rows):
            copy2(q, d).wait()
            total = total + got2[q, d]
        binned = total.astype(bf16)
        for f in range(share):
            power = jnp.dot(binned[f * cols:(f + 1) * cols], kern[q, f], preferred_element_type=f32)
            power = power * lax.rsqrt(jnp.mean(power * power, axis=1, keepdims=True) + 1e-06)
            for k in range(cols):
                ready[k, q * share + f:q * share + f + 1, :] = power[k:k + 1]

    def copy3(d):
        to = lax.rem(c + d, cols)
        return pltpu.make_async_remote_copy(
            ready.at[to], got3.at[d], send3.at[d], recv3.at[d], device_id=(r, to), device_id_type=MESH)

    def put(source, block):
        for q in range(HALVES):
            for f in range(share):
                out_ref[0, pl.ds(q * half + source * share + f, 1), :] = block[q * share + f:q * share + f + 1]

    for d in range(1, cols):
        copy3(d).start()
    put(c, ready[c])
    for d in range(1, cols):
        copy3(d).wait()
        put(lax.rem(c - d + cols, cols), got3[d])
    for k in range(PIECES):
        sib_copy(k).wait_send()
        for d in range(1, pairs):
            row_copy(d, k).wait_send()
            fwd_copy(d, k).wait_send()
        for d in range(1, rows):
            for way in (1, -1):
                made = col_send_copy(way, d, k)
                pl.when(made[0])(made[1].wait_send)


def on_device(spectra, pair_bins, row_subs, station_subs, kernel):
    shard, freqs, width = spectra.shape
    rows, cols = lax.axis_size("row"), lax.axis_size("col")
    span, group = pair_bins.shape
    slots = row_subs.shape[1]
    half = freqs // HALVES
    share = half // cols
    depth = slots * share
    speeds = kernel.shape[2]
    pairs = cols // 2
    dma = pltpu.SemaphoreType.DMA
    vmem = pl.BlockSpec(memory_space=pltpu.VMEM)
    bf16, f32 = jnp.bfloat16, jnp.float32
    return pl.pallas_call(
        functools.partial(body, rows, cols),
        out_shape=jax.ShapeDtypeStruct((1, freqs, speeds), f32),
        in_specs=[vmem, vmem, pl.BlockSpec(memory_space=pltpu.SMEM), vmem, pl.BlockSpec(memory_space=pl.ANY)],
        out_specs=vmem,
        scratch_shapes=[
            pltpu.VMEM((shard * freqs, width), f32),
            pltpu.VMEM((freqs, shard, width), bf16),
            pltpu.VMEM((freqs, cols * shard, width), bf16),
            pltpu.VMEM((freqs, rows * shard, width), bf16),
            pltpu.VMEM((slots, station_subs.shape[0]), f32),
            pltpu.VMEM((span, slots, group), bf16),
            pltpu.VMEM((span // UNROLL, NBIN, UNROLL * group), bf16),
            pltpu.VMEM((span * freqs, group), f32),
            pltpu.VMEM((slots * half, UNROLL * group), bf16),
            pltpu.VMEM((slots * half, UNROLL * group), bf16),
            pltpu.VMEM((slots * half, NBIN), f32),
            pltpu.VMEM((HALVES, cols, depth, NBIN), f32),
            pltpu.VMEM((HALVES, cols, depth, NBIN), f32),
            pltpu.VMEM((HALVES, rows, share * cols, NBIN), f32),
            pltpu.VMEM((HALVES, rows, share * cols, NBIN), f32),
            pltpu.VMEM((cols, HALVES * share, speeds), f32),
            pltpu.VMEM((cols, HALVES * share, speeds), f32),
            pltpu.VMEM((HALVES, share, NBIN, speeds), bf16),
            dma((2,)), dma((HALVES,)),
            dma((pairs, PIECES)), dma((pairs, PIECES)), dma((PIECES,)), dma((PIECES,)),
            dma((pairs, PIECES)), dma((pairs, PIECES)),
            dma((2, rows, PIECES)), dma((2, rows, PIECES)),
            dma((HALVES, cols)), dma((HALVES, cols)), dma((HALVES, rows)), dma((HALVES, rows)),
            dma((cols,)), dma((cols,)),
        ],
        compiler_params=pltpu.CompilerParams(collective_id=0, has_side_effects=True, vmem_limit_bytes=62 << 20),
        name="dispersion",
    )(spectra, pair_bins, row_subs, station_subs.T, kernel)


def solution(mesh):
    in_specs = (P(("row", "col"), None, None), P("row", "col"), P("row", None), P(), P())
    out_specs = P(("row", "col"), None, None)
    return jax.shard_map(
        on_device, mesh=mesh, in_specs=in_specs, out_specs=out_specs, check_vma=False
    )
```
